32 devices in a mesh: prop: 8 (over y, x, core), width: 4 (over z).
Axes of the slice: x: 2, y: 2, z: 4, core: 2. Of those that a mesh axis runs over, the one named last changes fastest.
Arguments:
- e_forward: float32 [3, 128, 128, 512], P(None, 'prop', 'width'), may hold values from -6 to 6
- h_forward: float32 [3, 128, 128, 512], P(None, 'prop', 'width'), may hold values from -6 to 6
- e_adjoint: float32 [3, 128, 128, 512], P(None, 'prop', 'width'), may hold values from -6 to 6
- h_adjoint: float32 [3, 128, 128, 512], P(None, 'prop', 'width'), may hold values from -6 to 6
- material: int32 [128, 128, 512], P('prop', 'width'), may hold values from 0 to 3
- eps_table: float32 [4], replicated, may hold values from 1.5 to 12
- omega: float32 [12], replicated, may hold values from 0.2 to 3
- mode_profile: float32 [64, 128, 512], P(None, 'width'), may hold values from -0.0234375 to 0.0234375
- port_order: int32 [64], replicated, may hold values from 0 to 63, each once
- owner: int32 [65536, 1], P(('prop', 'width')), may hold values from 0 to 31; in each aligned block of 2048 rows (0 to 2047, 2048 to 4095, ...) at most 128 rows name the same one
- segment: int32 [65536], P(('prop', 'width')), may hold values from 0 to 7
Outputs:
- e_forward_end: float32 [3, 128, 128, 512], P(None, 'prop', 'width')
- e_adjoint_end: float32 [3, 128, 128, 512], P(None, 'prop', 'width')
- port_amp: float32 [8, 64, 24], P('prop', 'width')
- seg_grad: float32 [256, 128], P(('prop', 'width'))
The draws below stay inside these ranges and needn't reach their ends.
Inputs may be any that keep to these rules, and one draw needn't show every extreme that they name: Among the 2048 blocks of one device, no owner is named more than 128 times, a bound that some block reaches. `port_order`: each port appears once.
All inputs are finite; a program needn't handle non-finite values.
Results may differ from the reference program's by a relative error of at most 0.0001.
Values sent between devices are 32-bit elements; how exact they have to be, the bound alone decides.
A program may use at most 128 MiB of HBM per device.

```python
import math
import jax
import jax.numpy as jnp
import numpy as np
from jax import lax

CX = 16
CY = 32
NZ = 512
STEPS = 2
NF = 12
NPORT = 64
NMAT = 4
ZBLK = 128
SEG_DEV = 8
NX = 128
NY = 128
BLK_DEV = 2048
ROWS = 65536
CAP = 128
N_PROP = 8
N_WIDTH = 4
DEVICES = 32


def set_ends(drawn, stream_key, low, largest):
    longest = drawn.shape.index(max(drawn.shape))
    spots = []
    for shift in (0, 1):
        where = [jax.random.randint(jax.random.fold_in(stream_key, axis), (), 0, length) for axis, length in enumerate(drawn.shape)]
        where[longest] = (where[longest] + shift) % drawn.shape[longest]
        spots.append(tuple(where))
    return drawn.at[spots[0]].set(low).at[spots[1]].set(largest)


def shard_levels(key, dims, cuts, smallest, top_value):
    def one(position, shards_of):
        heights = jax.random.uniform(jax.random.fold_in(jax.random.fold_in(key, 6), position), (shards_of,), jnp.float32, smallest / len(cuts), top_value / len(cuts))
        return jnp.repeat(jnp.exp(heights), dims[position] // shards_of).reshape((-1,) + (1,) * (len(dims) - position - 1))

    loudness = one(*cuts[0])
    for cut in cuts[1:]:
        loudness = loudness * one(*cut)
    return loudness


def shared_out(own_key, own, number, rows, amount, top, bound, slope):
    ranking = jax.random.permutation(own_key, amount)
    crowded, usual = portions_of(amount, rows * top, bound, slope, True), portions_of(amount, rows * top, bound, slope, False)
    places = jnp.arange(amount)

    def named(sizes, turn):
        used = int((sizes > 0).sum())
        fixed = max(1, used // 4)
        shifted = fixed + (places - fixed + turn * (used - fixed)) % max(1, amount - fixed)
        return jnp.zeros((amount,), jnp.int32).at[ranking[jnp.where(places < fixed, places, shifted)]].set(jnp.asarray(sizes, jnp.int32))

    sizes = jnp.where(number % 4 == 0, named(crowded, number // 4), named(usual, number - number // 4 - 1))
    mixed = jax.random.permutation(jax.random.fold_in(own, 3), amount)
    donor, taker = mixed[0:amount // 2 * 2:2], mixed[1:amount // 2 * 2:2]
    margin = jnp.minimum(sizes[donor] - 1, bound - sizes[taker]) // 2
    margin = jnp.where((donor == ranking[0]) | (taker == ranking[0]) | (sizes[taker] == 0), 0, jnp.maximum(margin, 0))
    shifted = jax.random.randint(jax.random.fold_in(own, 4), (amount // 2,), 0, 1 << 20) % (margin + 1)
    sizes = sizes.at[donor].add(-shifted).at[taker].add(shifted)
    members = jnp.searchsorted(jnp.cumsum(sizes), jnp.arange(rows * top), side="right").astype(jnp.int32)
    table = members.reshape(top, rows).T
    table = table[jax.random.permutation(jax.random.fold_in(own, 1), rows)]
    turn = jax.random.randint(jax.random.fold_in(own, 2), (rows, 1), 0, top)
    return jnp.take_along_axis(table, (jnp.arange(top)[None, :] + turn) % top, axis=1)


def portions_of(number_of, total, most, skew, full):
    loads = [(1 << 20) // math.isqrt(grade ** skew) + 1 for grade in range(1, number_of + 1)]
    largest = most if full else min(most, max(-(-total // number_of), total * loads[0] // sum(loads)))
    least = 1 if total - largest >= number_of - 1 else 0
    counts, surplus = [largest] + [least] * (number_of - 1), total - largest - least * (number_of - 1)
    while surplus > 0:
        candidates = [i for i in range(1, number_of) if counts[i] < largest] or [i for i in range(1, number_of) if counts[i] < most]
        whole, remaining = sum([loads[i] for i in candidates]), surplus
        for i in candidates:
            more = min(most - counts[i], max(1, remaining * loads[i] // whole), surplus)
            counts[i] = counts[i] + more
            surplus = surplus - more
    return np.array(counts)


def normal_values(stream_key, extent, spread, bound, shards=(), held_as=jnp.bfloat16):
    gain = shard_levels(stream_key, extent, shards, -0.22, 0.18) if shards else 1.0
    values = jax.random.normal(stream_key, extent, jnp.float32) * spread * gain
    return jnp.minimum(jnp.maximum(values, -bound), bound).astype(held_as)


def setup_inputs(seed: int = 0) -> dict:
    keys = jax.random.split(jax.random.key(seed), 12)
    e_forward = normal_values(keys[0], (3, NX, NY, NZ), 1.0, 6.0, ((1, 8), (2, 4)), jnp.float32)
    h_forward = normal_values(keys[1], (3, NX, NY, NZ), 1.0, 6.0, ((1, 8), (2, 4)), jnp.float32)
    e_adjoint = normal_values(keys[2], (3, NX, NY, NZ), 1.0, 6.0, ((1, 8), (2, 4)), jnp.float32)
    h_adjoint = normal_values(keys[3], (3, NX, NY, NZ), 1.0, 6.0, ((1, 8), (2, 4)), jnp.float32)
    material = set_ends(jax.random.randint(keys[4], (NX, NY, NZ), 0, NMAT), jax.random.fold_in(keys[4], 1), 0, NMAT - 1).astype(jnp.int32)
    eps_table = jnp.clip(jax.random.uniform(keys[5], (NMAT,), jnp.float32, 1.5, 12.0), 1.5, 12.0)
    omega = jnp.clip(jnp.exp(jax.random.uniform(keys[6], (NF,), jnp.float32, math.log(0.2), math.log(3.0))), 0.2, 3.0)
    mode_profile = normal_values(keys[7], (NPORT, NY, NZ), (NY * NZ) ** -0.5, 0.0234375, ((1, 4),), jnp.float32)
    port_order = jax.random.permutation(keys[8], NPORT).astype(jnp.int32)
    owner_keys = jax.random.split(jax.random.fold_in(keys[9], 1), ROWS // BLK_DEV)
    owner_turns = jax.random.permutation(jax.random.fold_in(keys[9], 3), ROWS // BLK_DEV)
    owner = jax.vmap(lambda own, number: shared_out(jax.random.fold_in(keys[9], 2), own, number, BLK_DEV, DEVICES, 1, CAP, 2))(owner_keys, owner_turns).reshape((ROWS, 1))
    segment = set_ends(jax.random.randint(keys[10], (ROWS,), 0, SEG_DEV), jax.random.fold_in(keys[10], 1), 0, SEG_DEV - 1).astype(jnp.int32)
    return dict(e_forward=e_forward, h_forward=h_forward, e_adjoint=e_adjoint, h_adjoint=h_adjoint, material=material, eps_table=eps_table, omega=omega, mode_profile=mode_profile, port_order=port_order, owner=owner, segment=segment)


COURANT = 0.5
GRAD_SCALE = -0.05


def ahead(field, face, axis):
    moved = jnp.concatenate([lax.slice_in_dim(field, 1, field.shape[axis], axis=axis), jnp.expand_dims(face, axis)], axis=axis)
    return moved - field


def behind(field, face, axis):
    moved = jnp.concatenate([jnp.expand_dims(face, axis), lax.slice_in_dim(field, 0, field.shape[axis] - 1, axis=axis)], axis=axis)
    return field - moved


def update_h(efield, hfield, face_x, face_y):
    ex_c, ey_c, ez_c = efield[:, 0], efield[:, 1], efield[:, 2]
    flat = jnp.zeros_like(ex_c[:, :, :, 0])
    curl_x = ahead(ez_c, face_y[:, 1], 2) - ahead(ey_c, flat, 3)
    curl_y = ahead(ex_c, flat, 3) - ahead(ez_c, face_x[:, 1], 1)
    curl_z = ahead(ey_c, face_x[:, 0], 1) - ahead(ex_c, face_y[:, 0], 2)
    return hfield - COURANT * jnp.stack([curl_x, curl_y, curl_z], axis=1)


def update_e(efield, hfield, coef, face_x, face_y):
    hx_c, hy_c, hz_c = hfield[:, 0], hfield[:, 1], hfield[:, 2]
    flat = jnp.zeros_like(hx_c[:, :, :, 0])
    curl_x = behind(hz_c, face_y[:, 1], 2) - behind(hy_c, flat, 3)
    curl_y = behind(hx_c, flat, 3) - behind(hz_c, face_x[:, 1], 1)
    curl_z = behind(hy_c, face_x[:, 0], 1) - behind(hx_c, face_y[:, 0], 2)
    return efield + coef[None, None] * jnp.stack([curl_x, curl_y, curl_z], axis=1)


def coefficient(material, eps_table):
    inverse = COURANT / eps_table
    coef = jnp.zeros(material.shape, jnp.float32)
    for which in range(NMAT):
        coef = coef + jnp.where(material == which, inverse[which], jnp.float32(0.0))
    return coef


def run_steps(efield, hfield, coef):
    face_x = jnp.zeros((1, 2, NY, NZ), jnp.float32)
    face_y = jnp.zeros((1, 2, NX, NZ), jnp.float32)
    history = []
    for step in range(STEPS):
        hfield = update_h(efield, hfield, face_x, face_y)
        efield = update_e(efield, hfield, coef, face_x, face_y)
        history.append(efield[0])
    return history


def reference(e_forward, h_forward, e_adjoint, h_adjoint, material, eps_table, omega, mode_profile, port_order, owner, segment):
    coef = coefficient(material, eps_table)
    fwd = run_steps(e_forward[None], h_forward[None], coef)
    adj = run_steps(e_adjoint[None], h_adjoint[None], coef)
    real_sum = None
    imag_sum = None
    for step in range(STEPS):
        plane = fwd[step][2, ::CX]
        angle = omega * jnp.float32(step + 1)
        real_term = jnp.cos(angle)[:, None, None, None] * plane[None]
        imag_term = jnp.sin(angle)[:, None, None, None] * plane[None]
        real_sum = real_term if real_sum is None else real_sum + real_term
        imag_sum = imag_term if imag_sum is None else imag_sum + imag_term
    dft = jnp.concatenate([real_sum, -imag_sum], axis=0).reshape(2 * NF, N_PROP, NY * NZ)
    amp = jnp.einsum("kpc,qc->pqk", dft, mode_profile.reshape(NPORT, NY * NZ), precision=lax.Precision.HIGHEST)
    port_amp = amp[:, port_order, :]
    total = None
    for step in range(STEPS):
        term = jnp.sum(fwd[step] * adj[STEPS - 1 - step], axis=0)
        total = term if total is None else total + term
    grad = GRAD_SCALE * total
    rows = grad.reshape(N_PROP, CX, N_WIDTH, CY, NZ // ZBLK, ZBLK).transpose(0, 2, 1, 3, 4, 5).reshape(-1, ZBLK)
    index = (owner[:, 0] * SEG_DEV + segment).astype(jnp.int32)
    seg_grad = jax.ops.segment_sum(rows, index, num_segments=N_PROP * N_WIDTH * SEG_DEV)
    return (fwd[STEPS - 1], adj[STEPS - 1], port_amp, seg_grad)
```

```python
import functools

import jax
import jax.numpy as jnp
from jax import lax
from jax.experimental import pallas as pl
from jax.experimental.pallas import tpu as pltpu
from jax.sharding import PartitionSpec as P

NMAT = 4
ZBLK = 128
SEG_DEV = 8
COURANT = 0.5
GRAD_SCALE = -0.05
MESH = pl.DeviceIdType.MESH
T = 8


def kernel(
    n_prop, n_width,
    ef_in, hf_in, ea_in, ha_in, mat_in, mode_in, eps_ref, omega_ref, order_ref, idx_ref,
    ef_out, ea_out, port_out, seg_out,
    E, H, E2, mat, coef, mode, hx_halo, hy_halo, ysend, G, OH, pacc,
    seg_part, recv1, part2, recv2, ordered, recvp,
    load_sem, out_sem, send_sem, recv_sem, red_send, red_recv,
):
    CX, CY, NZ = mat.shape
    TILES = CY // T
    ZB = NZ // ZBLK
    p = lax.axis_index("prop")
    w = lax.axis_index("width")
    e_in, h_in = (ef_in, ea_in), (hf_in, ha_in)

    loads_e = [pltpu.make_async_copy(e_in[r], E.at[r], load_sem.at[r]) for r in range(2)]
    loads_h = [pltpu.make_async_copy(h_in[r], H.at[r], load_sem.at[2 + r]) for r in range(2)]
    load_mat = pltpu.make_async_copy(mat_in, mat, load_sem.at[4])
    load_mode = pltpu.make_async_copy(mode_in, mode, load_sem.at[5])
    for c in loads_e + loads_h + [load_mat, load_mode]:
        c.start()

    barrier = pltpu.get_barrier_semaphore()
    for d in range(1, n_prop):
        pl.semaphore_signal(barrier, inc=1, device_id=(lax.rem(p + d, n_prop), w), device_id_type=MESH)
    for d in range(1, n_width):
        pl.semaphore_signal(barrier, inc=1, device_id=(p, lax.rem(w + d, n_width)), device_id_type=MESH)

    def sem_of(r, phase, direction):
        return (r * 4 + phase) * 2 + direction

    def face_copy(r, phase, direction):
        ahead = phase % 2 == 0
        step = -1 if ahead else 1
        if direction == 0:
            if phase == 0:
                src = e_in[r].at[pl.ds(1, 2), 0]
            elif ahead:
                src = E.at[r, pl.ds(1, 2), 0]
            else:
                src = H.at[r, pl.ds(1, 2), CX - 1]
            dst = hx_halo.at[r, phase]
            dev = (jnp.clip(p + step, 0, n_prop - 1), w)
            may_send = p > 0 if ahead else p < n_prop - 1
            may_recv = p < n_prop - 1 if ahead else p > 0
        else:
            src = ysend.at[r, phase]
            dst = hy_halo.at[r, phase]
            dev = (p, jnp.clip(w + step, 0, n_width - 1))
            may_send = w > 0 if ahead else w < n_width - 1
            may_recv = w < n_width - 1 if ahead else w > 0
        k = sem_of(r, phase, direction)
        copy = pltpu.make_async_remote_copy(
            src_ref=src, dst_ref=dst, send_sem=send_sem.at[k], recv_sem=recv_sem.at[k],
            device_id=dev, device_id_type=MESH,
        )
        return copy, may_send, may_recv

    def send(r, phase, direction):
        copy, may_send, _ = face_copy(r, phase, direction)

        @pl.when(may_send)
        def _():
            copy.start()

    def wait_send(r, phase, direction):
        copy, may_send, _ = face_copy(r, phase, direction)

        @pl.when(may_send)
        def _():
            copy.wait_send()

    def wait_recv(r, phase, direction):
        copy, _, may_recv = face_copy(r, phase, direction)

        @pl.when(may_recv)
        def _():
            copy.wait_recv()

        @pl.when(jnp.logical_not(may_recv))
        def _():
            if direction == 0:
                hx_halo[r, phase] = jnp.zeros(hx_halo.shape[2:], jnp.float32)
            else:
                hy_halo[r, phase] = jnp.zeros(hy_halo.shape[2:], jnp.float32)

    row = lax.broadcasted_iota(jnp.int32, (T, NZ), 0)
    lane = lax.broadcasted_iota(jnp.int32, (T, NZ), 1)
    row_last, row_first = row == T - 1, row == 0
    lane_last, lane_first = lane == NZ - 1, lane == 0
    zero = jnp.float32(0.0)

    def z_next(v):
        return jnp.where(lane_last, zero, pltpu.roll(v, NZ - 1, 1))

    def z_prev(v):
        return jnp.where(lane_first, zero, pltpu.roll(v, 1, 1))

    def y_next(v, nxt):
        return jnp.where(row_last, jnp.broadcast_to(nxt, v.shape), pltpu.roll(v, T - 1, 0))

    def y_prev(v, prv):
        return jnp.where(row_first, jnp.broadcast_to(prv, v.shape), pltpu.roll(v, 1, 0))

    def h_tile(r, phase, i, j, x_edge):
        rows = pl.ds(j * T, T)
        ex, ey, ez = E[r, 0, i, rows, :], E[r, 1, i, rows, :], E[r, 2, i, rows, :]
        if x_edge:
            ey_x, ez_x = hx_halo[r, phase, 0, rows, :], hx_halo[r, phase, 1, rows, :]
        else:
            ey_x, ez_x = E[r, 1, i + 1, rows, :], E[r, 2, i + 1, rows, :]
        if j == TILES - 1:
            nx, nz = hy_halo[r, phase, 0, i], hy_halo[r, phase, 1, i]
        else:
            nx, nz = E[r, 0, i, pl.ds(j * T + T, 1), :], E[r, 2, i, pl.ds(j * T + T, 1), :]
        cx = (y_next(ez, nz) - ez) - (z_next(ey) - ey)
        cy = (z_next(ex) - ex) - (ez_x - ez)
        cz = (ey_x - ey) - (y_next(ex, nx) - ex)
        H[r, 0, i, rows, :] = H[r, 0, i, rows, :] - COURANT * cx
        H[r, 1, i, rows, :] = H[r, 1, i, rows, :] - COURANT * cy
        H[r, 2, i, rows, :] = H[r, 2, i, rows, :] - COURANT * cz

    def e_tile(r, phase, i, j, x_edge):
        rows = pl.ds(j * T, T)
        hx, hy, hz = H[r, 0, i, rows, :], H[r, 1, i, rows, :], H[r, 2, i, rows, :]
        if x_edge:
            hy_x, hz_x = hx_halo[r, phase, 0, rows, :], hx_halo[r, phase, 1, rows, :]
        else:
            hy_x, hz_x = H[r, 1, i - 1, rows, :], H[r, 2, i - 1, rows, :]
        if j == 0:
            px, pz = hy_halo[r, phase, 0, i], hy_halo[r, phase, 1, i]
        else:
            px, pz = H[r, 0, i, pl.ds(j * T - 1, 1), :], H[r, 2, i, pl.ds(j * T - 1, 1), :]
        k = coef[i, rows, :]
        old = [E[r, c, i, rows, :] for c in range(3)]
        new = [
            old[0] + k * ((hz - y_prev(hz, pz)) - (hy - z_prev(hy))),
            old[1] + k * ((hx - z_prev(hx)) - (hz - hz_x)),
            old[2] + k * ((hy - hy_x) - (hx - y_prev(hx, px))),
        ]
        out = E if phase == 1 else E2
        for c in range(3):
            out[r, c, i, rows, :] = new[c]
        if phase == 3 and r == 1:
            total = None
            for c in range(3):
                term = E[0, c, i, rows, :] * new[c] + E2[0, c, i, rows, :] * old[c]
                total = term if total is None else total + term
            g = GRAD_SCALE * total
            for z in range(ZB):
                G[pl.ds((i * CY + j * T) * ZB + z, T, stride=ZB), :] = g[:, z * ZBLK:(z + 1) * ZBLK]

    def h_inner(r, phase):
        def body(i, carry):
            for j in range(TILES - 1):
                h_tile(r, phase, i, j, False)
            return carry

        lax.fori_loop(0, CX - 1, body, 0)

    def h_edge(r, phase, save):
        def body(i, carry):
            h_tile(r, phase, i, TILES - 1, False)
            for n, c in enumerate((0, 2)):
                ysend[r, phase + 1, n, i] = H[r, c, i, pl.ds(CY - 1, 1), :]
            return carry

        for j in range(TILES):
            h_tile(r, phase, CX - 1, j, True)
        for n, c in enumerate((0, 2)):
            ysend[r, phase + 1, n, CX - 1] = H[r, c, CX - 1, pl.ds(CY - 1, 1), :]
        send(r, phase + 1, 0)
        lax.fori_loop(0, CX - 1, body, 0)
        send(r, phase + 1, 1)

    def e_inner(r, phase):
        def body(i, carry):
            for j in range(1, TILES):
                e_tile(r, phase, i, j, False)
            return carry

        lax.fori_loop(1, CX, body, 0)

    def e_edge(r, phase):
        more = phase == 1

        def body(i, carry):
            e_tile(r, phase, i, 0, False)
            if more:
                for n, c in enumerate((0, 2)):
                    ysend[r, phase + 1, n, i] = E[r, c, i, pl.ds(0, 1), :]
            return carry

        for j in range(TILES):
            e_tile(r, phase, 0, j, True)
        if more:
            for n, c in enumerate((0, 2)):
                ysend[r, phase + 1, n, 0] = E[r, c, 0, pl.ds(0, 1), :]
            send(r, phase + 1, 0)
        lax.fori_loop(1, CX, body, 0)
        if more:
            send(r, phase + 1, 1)

    def ports(fields, t):
        plane = [fields[0, 2, 0, pl.ds(j * T, T), :] for j in range(TILES)]

        def body(q, carry):
            acc = None
            for j in range(TILES):
                m = mode[q, pl.ds(j * T, T), :] * plane[j]
                acc = m if acc is None else acc + m
            total = acc[:, :ZBLK]
            for z in range(1, ZB):
                total = total + acc[:, z * ZBLK:(z + 1) * ZBLK]
            pacc[pl.ds(pl.multiple_of(q * T, T), T), pl.ds(t * ZBLK, ZBLK)] = total
            return carry

        lax.fori_loop(0, mode.shape[0], body, 0)

    pl.semaphore_wait(barrier, n_prop + n_width - 2)
    for r in range(2):
        send(r, 0, 0)
    for r in range(2):
        loads_e[r].wait()

        def rows_out(i, carry, r=r):
            for n, c in enumerate((0, 2)):
                ysend[r, 0, n, i] = E[r, c, i, pl.ds(0, 1), :]
            return carry

        lax.fori_loop(0, CX, rows_out, 0)
        send(r, 0, 1)

    load_mat.wait()

    def coef_body(i, carry):
        inv = [COURANT / jnp.full((T, NZ), eps_ref[m], jnp.float32) for m in range(NMAT)]
        for j in range(TILES):
            v = mat[i, pl.ds(j * T, T), :]
            out = jnp.zeros((T, NZ), jnp.float32)
            for m in range(NMAT):
                out = jnp.where(v == m, inv[m], out)
            coef[i, pl.ds(j * T, T), :] = out
        return carry

    lax.fori_loop(0, CX, coef_body, 0)

    loads_h[0].wait()
    h_inner(0, 0)
    loads_h[1].wait()
    h_inner(1, 0)

    for step in range(2):
        a, b = 2 * step, 2 * step + 1
        if step == 1:
            for r in range(2):
                h_inner(r, a)
        for r in range(2):
            wait_recv(r, a, 0)
            wait_recv(r, a, 1)
            if step == 1:
                wait_send(r, 1, 0)
            h_edge(r, a, True)
        for r in range(2):
            e_inner(r, b)
        if step == 0:
            def hot(s, carry):
                base = pl.multiple_of(s * 32, 32)
                mine = lax.broadcasted_iota(jnp.int32, (32, idx_ref.shape[1]), 0) + base
                OH[pl.ds(base, 32), :] = jnp.where(mine == idx_ref[...], 1.0, 0.0).astype(jnp.bfloat16)
                return carry

            lax.fori_loop(0, OH.shape[0] // 32, hot, 0)
        for r in range(2):
            wait_recv(r, b, 0)
            wait_recv(r, b, 1)
            if step == 0:
                pass
            e_edge(r, b)
            if step == 1:
                pltpu.make_async_copy(E2.at[r], (ef_out, ea_out)[r], out_sem.at[r]).start()
        if step == 0:
            load_mode.wait()
            ports(E, 0)
    seg = None
    K = 512
    for k in range(G.shape[0] // K):
        g = G[pl.ds(k * K, K), :]
        hi = g.astype(jnp.bfloat16)
        lo = (g - hi.astype(jnp.float32)).astype(jnp.bfloat16)
        part = OH[:, pl.ds(k * K, K)]
        term = jnp.dot(part, hi, preferred_element_type=jnp.float32) + jnp.dot(part, lo, preferred_element_type=jnp.float32)
        seg = term if seg is None else seg + term
    seg_part[...] = seg.reshape(seg_part.shape)

    def width_copies(d):
        to = lax.rem(w + d, n_width)
        seg_c = pltpu.make_async_remote_copy(
            src_ref=seg_part.at[:, to], dst_ref=recv1.at[d - 1],
            send_sem=red_send.at[d - 1], recv_sem=red_recv.at[d - 1],
            device_id=(p, to), device_id_type=MESH)
        port_c = pltpu.make_async_remote_copy(
            src_ref=ordered.at[to], dst_ref=recvp.at[d - 1],
            send_sem=red_send.at[n_width - 1 + d - 1], recv_sem=red_recv.at[n_width - 1 + d - 1],
            device_id=(p, to), device_id_type=MESH)
        return seg_c, port_c

    for d in range(1, n_width):
        width_copies(d)[0].start()

    ports(E2, 1)
    n_ports = mode.shape[0]
    port_of = lax.broadcasted_iota(jnp.int32, (n_ports, n_ports * T), 1) // T
    pick = jnp.where(port_of == order_ref[...], 1.0, 0.0).astype(jnp.bfloat16)
    v = pacc[...]
    hi = v.astype(jnp.bfloat16)
    lo = (v - hi.astype(jnp.float32)).astype(jnp.bfloat16)
    o = jnp.dot(pick, hi, preferred_element_type=jnp.float32) + jnp.dot(pick, lo, preferred_element_type=jnp.float32)
    ordered[...] = o.reshape(ordered.shape)
    for d in range(1, n_width):
        width_copies(d)[1].start()

    for d in range(1, n_width):
        width_copies(d)[0].wait_recv()
    total = seg_part[:, w]
    for d in range(1, n_width):
        total = total + recv1[d - 1]
    part2[...] = total

    base = 2 * (n_width - 1)

    def prop_copy(d):
        to = lax.rem(p + d, n_prop)
        return pltpu.make_async_remote_copy(
            src_ref=part2.at[to], dst_ref=recv2.at[d - 1],
            send_sem=red_send.at[base + d - 1], recv_sem=red_recv.at[base + d - 1],
            device_id=(to, w), device_id_type=MESH)

    for d in range(1, n_prop):
        prop_copy(d).start()

    for d in range(1, n_width):
        width_copies(d)[1].wait_recv()
    mine = ordered[w]
    for d in range(1, n_width):
        mine = mine + recvp[d - 1]
    s1 = jnp.sum(mine[:, :ZBLK], axis=1, keepdims=True)
    s2 = jnp.sum(mine[:, ZBLK:], axis=1, keepdims=True)
    nf = omega_ref.shape[1]
    om = jnp.broadcast_to(omega_ref[...], (mine.shape[0], nf))
    port_out[0, :, 0:nf] = jnp.cos(om) * s1 + jnp.cos(om * 2.0) * s2
    port_out[0, :, nf:2 * nf] = -(jnp.sin(om) * s1 + jnp.sin(om * 2.0) * s2)

    for d in range(1, n_prop):
        prop_copy(d).wait_recv()
    got = part2[p]
    for d in range(1, n_prop):
        got = got + recv2[d - 1]
    seg_out[...] = got

    for r in range(2):
        for phase in range(4):
            for direction in range(2):
                if (phase, direction) != (1, 0):
                    wait_send(r, phase, direction)
    for d in range(1, n_width):
        width_copies(d)[0].wait_send()
        width_copies(d)[1].wait_send()
    for d in range(1, n_prop):
        prop_copy(d).wait_send()
    for r in range(2):
        pltpu.make_async_copy(E2.at[r], (ef_out, ea_out)[r], out_sem.at[r]).wait()


def on_device(
    n_prop, n_width,
    e_forward, h_forward, e_adjoint, h_adjoint, material, eps_table, omega,
    mode_profile, port_order, owner, segment,
):
    _, CX, CY, NZ = e_forward.shape
    blocks = owner.shape[0]
    ports = mode_profile.shape[0]
    nf = omega.shape[0]
    segs = n_prop * n_width * SEG_DEV
    idx = owner.reshape(1, blocks) * SEG_DEV + segment.reshape(1, blocks)
    anyspec = pl.BlockSpec(memory_space=pl.ANY)
    vm = pl.BlockSpec(memory_space=pltpu.VMEM)
    sm = pl.BlockSpec(memory_space=pltpu.SMEM)
    f32 = jnp.float32
    n_red = 2 * (n_width - 1) + n_prop - 1
    field = (2, 3, CX, CY, NZ)
    return pl.pallas_call(
        functools.partial(kernel, n_prop, n_width),
        out_shape=(
            jax.ShapeDtypeStruct(e_forward.shape, f32),
            jax.ShapeDtypeStruct(e_adjoint.shape, f32),
            jax.ShapeDtypeStruct((1, ports // n_width, 2 * nf), f32),
            jax.ShapeDtypeStruct((SEG_DEV, ZBLK), f32),
        ),
        in_specs=[anyspec] * 6 + [sm, vm, vm, vm],
        out_specs=(anyspec, anyspec, vm, vm),
        scratch_shapes=[
            pltpu.VMEM(field, f32),
            pltpu.VMEM(field, f32),
            pltpu.VMEM(field, f32),
            pltpu.VMEM((CX, CY, NZ), jnp.int32),
            pltpu.VMEM((CX, CY, NZ), f32),
            pltpu.VMEM((ports, CY, NZ), f32),
            pltpu.VMEM((2, 4, 2, CY, NZ), f32),
            pltpu.VMEM((2, 4, 2, CX, 1, NZ), f32),
            pltpu.VMEM((2, 4, 2, CX, 1, NZ), f32),
            pltpu.VMEM((blocks, ZBLK), f32),
            pltpu.VMEM((segs, blocks), jnp.bfloat16),
            pltpu.VMEM((ports * T, 2 * ZBLK), f32),
            pltpu.VMEM((n_prop, n_width, SEG_DEV, ZBLK), f32),
            pltpu.VMEM((n_width - 1, n_prop, SEG_DEV, ZBLK), f32),
            pltpu.VMEM((n_prop, SEG_DEV, ZBLK), f32),
            pltpu.VMEM((n_prop - 1, SEG_DEV, ZBLK), f32),
            pltpu.VMEM((n_width, ports // n_width, 2 * ZBLK), f32),
            pltpu.VMEM((n_width - 1, ports // n_width, 2 * ZBLK), f32),
            pltpu.SemaphoreType.DMA((6,)),
            pltpu.SemaphoreType.DMA((2,)),
            pltpu.SemaphoreType.DMA((16,)),
            pltpu.SemaphoreType.DMA((16,)),
            pltpu.SemaphoreType.DMA((n_red,)),
            pltpu.SemaphoreType.DMA((n_red,)),
        ],
        compiler_params=pltpu.CompilerParams(
            collective_id=0, has_side_effects=True, vmem_limit_bytes=60 * 1024 * 1024
        ),
    )(
        e_forward, h_forward, e_adjoint, h_adjoint, material, mode_profile,
        eps_table, omega.reshape(1, nf), port_order.reshape(ports, 1), idx,
    )


def solution(mesh):
    n_prop, n_width = mesh.shape["prop"], mesh.shape["width"]
    placed = (
        P(None, "prop", "width", None),
        P(None, "prop", "width", None),
        P(None, "prop", "width", None),
        P(None, "prop", "width", None),
        P("prop", "width", None),
        P(),
        P(),
        P(None, "width", None),
        P(),
        P(("prop", "width"), None),
        P(("prop", "width")),
    )
    return jax.shard_map(
        functools.partial(on_device, n_prop, n_width),
        mesh=mesh,
        in_specs=placed,
        out_specs=(
            P(None, "prop", "width", None),
            P(None, "prop", "width", None),
            P("prop", "width", None),
            P(("prop", "width"), None),
        ),
        check_vma=False,
    )
```

```python
import functools

import jax
import jax.numpy as jnp
from jax import lax
from jax.experimental import pallas as pl
from jax.experimental.pallas import tpu as pltpu
from jax.sharding import PartitionSpec as P

NMAT = 4
ZBLK = 128
SEG_DEV = 8
COURANT = 0.5
GRAD_SCALE = -0.05
MESH = pl.DeviceIdType.MESH
T = 8


def kernel(
    n_prop, n_width,
    ef_in, hf_in, ea_in, ha_in, mat_in, mode_in, eps_ref, omega_ref, order_ref, owner_ref, segment_ref,
    E2, port_out, seg_out,
    E, H, mat, coef, mode, hx_halo, hy_halo, ysend, G, OH, pacc, trig,
    seg_part, recv1, part2, recv2, ordered, recvp,
    load_sem, send_sem, recv_sem, red_send, red_recv,
):
    CX, CY, NZ = mat.shape
    TILES = CY // T
    ZB = NZ // ZBLK
    p = lax.axis_index("prop")
    w = lax.axis_index("width")
    e_in, h_in = (ef_in, ea_in), (hf_in, ha_in)

    def load(src, dst, k):
        return pltpu.make_async_copy(src, dst, load_sem.at[k])

    first = [[load(e_in[r].at[c, :, pl.ds(0, T), :], E.at[r, c, :, pl.ds(0, T), :], r * 6 + n)
              for n, c in enumerate((0, 2))] for r in range(2)]
    rest = [[load(e_in[r].at[c, :, pl.ds(T, CY - T), :], E.at[r, c, :, pl.ds(T, CY - T), :], r * 6 + 2 + n)
             for n, c in enumerate((0, 2))] + [load(e_in[r].at[1], E.at[r, 1], r * 6 + 4)] for r in range(2)]
    loads_h = [load(h_in[r], H.at[r], r * 6 + 5) for r in range(2)]
    load_mat = load(mat_in, mat, 12)
    load_mode = load(mode_in, mode, 13)
    for c in first[0] + first[1] + rest[0] + [loads_h[0]]:
        c.start()

    barrier = pltpu.get_barrier_semaphore()
    for d in range(1, n_prop):
        pl.semaphore_signal(barrier, inc=1, device_id=(lax.rem(p + d, n_prop), w), device_id_type=MESH)
    for d in range(1, n_width):
        pl.semaphore_signal(barrier, inc=1, device_id=(p, lax.rem(w + d, n_width)), device_id_type=MESH)

    def sem_of(r, phase, direction):
        return (r * 4 + phase) * 2 + direction

    def face_copy(r, phase, direction):
        ahead = phase % 2 == 0
        step = -1 if ahead else 1
        if direction == 0:
            if phase == 0:
                src = e_in[r].at[pl.ds(1, 2), 0]
            elif ahead:
                src = E.at[r, pl.ds(1, 2), 0]
            else:
                src = H.at[r, pl.ds(1, 2), CX - 1]
            dst = hx_halo.at[r, phase]
            dev = (jnp.clip(p + step, 0, n_prop - 1), w)
            may_send = p > 0 if ahead else p < n_prop - 1
            may_recv = p < n_prop - 1 if ahead else p > 0
        else:
            src = ysend.at[r, phase]
            dst = hy_halo.at[r, phase]
            dev = (p, jnp.clip(w + step, 0, n_width - 1))
            may_send = w > 0 if ahead else w < n_width - 1
            may_recv = w < n_width - 1 if ahead else w > 0
        k = sem_of(r, phase, direction)
        copy = pltpu.make_async_remote_copy(
            src_ref=src, dst_ref=dst, send_sem=send_sem.at[k], recv_sem=recv_sem.at[k],
            device_id=dev, device_id_type=MESH,
        )
        return copy, may_send, may_recv

    def send(r, phase, direction):
        copy, may_send, _ = face_copy(r, phase, direction)

        @pl.when(may_send)
        def _():
            copy.start()

    def wait_send(r, phase, direction):
        copy, may_send, _ = face_copy(r, phase, direction)

        @pl.when(may_send)
        def _():
            copy.wait_send()

    def wait_recv(r, phase, direction):
        copy, _, may_recv = face_copy(r, phase, direction)

        @pl.when(may_recv)
        def _():
            copy.wait_recv()

        @pl.when(jnp.logical_not(may_recv))
        def _():
            if direction == 0:
                hx_halo[r, phase] = jnp.zeros(hx_halo.shape[2:], jnp.float32)
            else:
                hy_halo[r, phase] = jnp.zeros(hy_halo.shape[2:], jnp.float32)

    row = lax.broadcasted_iota(jnp.int32, (T, NZ), 0)
    lane = lax.broadcasted_iota(jnp.int32, (T, NZ), 1)
    row_last, row_first = row == T - 1, row == 0
    lane_last, lane_first = lane == NZ - 1, lane == 0
    zero = jnp.float32(0.0)

    def z_next(v):
        return jnp.where(lane_last, zero, pltpu.roll(v, NZ - 1, 1))

    def z_prev(v):
        return jnp.where(lane_first, zero, pltpu.roll(v, 1, 1))

    def y_next(v, nxt):
        return jnp.where(row_last, jnp.broadcast_to(nxt, v.shape), pltpu.roll(v, T - 1, 0))

    def y_prev(v, prv):
        return jnp.where(row_first, jnp.broadcast_to(prv, v.shape), pltpu.roll(v, 1, 0))

    def h_tile(r, phase, i, j, x_edge):
        rows = pl.ds(j * T, T)
        ex, ey, ez = E[r, 0, i, rows, :], E[r, 1, i, rows, :], E[r, 2, i, rows, :]
        if x_edge:
            ey_x, ez_x = hx_halo[r, phase, 0, rows, :], hx_halo[r, phase, 1, rows, :]
        else:
            ey_x, ez_x = E[r, 1, i + 1, rows, :], E[r, 2, i + 1, rows, :]
        if j == TILES - 1:
            nx, nz = hy_halo[r, phase, 0, i], hy_halo[r, phase, 1, i]
        else:
            nx, nz = E[r, 0, i, pl.ds(j * T + T, 1), :], E[r, 2, i, pl.ds(j * T + T, 1), :]
        cx = (y_next(ez, nz) - ez) - (z_next(ey) - ey)
        cy = (z_next(ex) - ex) - (ez_x - ez)
        cz = (ey_x - ey) - (y_next(ex, nx) - ex)
        H[r, 0, i, rows, :] = H[r, 0, i, rows, :] - COURANT * cx
        H[r, 1, i, rows, :] = H[r, 1, i, rows, :] - COURANT * cy
        H[r, 2, i, rows, :] = H[r, 2, i, rows, :] - COURANT * cz

    def e_tile(r, phase, i, j, x_edge):
        rows = pl.ds(j * T, T)
        hx, hy, hz = H[r, 0, i, rows, :], H[r, 1, i, rows, :], H[r, 2, i, rows, :]
        if x_edge:
            hy_x, hz_x = hx_halo[r, phase, 0, rows, :], hx_halo[r, phase, 1, rows, :]
        else:
            hy_x, hz_x = H[r, 1, i - 1, rows, :], H[r, 2, i - 1, rows, :]
        if j == 0:
            px, pz = hy_halo[r, phase, 0, i], hy_halo[r, phase, 1, i]
        else:
            px, pz = H[r, 0, i, pl.ds(j * T - 1, 1), :], H[r, 2, i, pl.ds(j * T - 1, 1), :]
        k = coef[i, rows, :]
        old = [E[r, c, i, rows, :] for c in range(3)]
        new = [
            old[0] + k * ((hz - y_prev(hz, pz)) - (hy - z_prev(hy))),
            old[1] + k * ((hx - z_prev(hx)) - (hz - hz_x)),
            old[2] + k * ((hy - hy_x) - (hx - y_prev(hx, px))),
        ]
        out = E if phase == 1 else E2
        for c in range(3):
            out[r, c, i, rows, :] = new[c]
        if phase == 3 and r == 1:
            total = None
            for c in range(3):
                term = E[0, c, i, rows, :] * new[c] + E2[0, c, i, rows, :] * old[c]
                total = term if total is None else total + term
            g = GRAD_SCALE * total
            for z in range(ZB):
                G[pl.ds((i * CY + j * T) * ZB + z, T, stride=ZB), :] = g[:, z * ZBLK:(z + 1) * ZBLK]

    def h_inner(r, phase):
        def body(i, carry):
            for j in range(TILES - 1):
                h_tile(r, phase, i, j, False)
            return carry

        lax.fori_loop(0, CX - 1, body, 0)

    def h_edge(r, phase):
        def body(i, carry):
            h_tile(r, phase, i, TILES - 1, False)
            for n, c in enumerate((0, 2)):
                ysend[r, phase + 1, n, i] = H[r, c, i, pl.ds(CY - 1, 1), :]
            return carry

        for j in range(TILES):
            h_tile(r, phase, CX - 1, j, True)
        for n, c in enumerate((0, 2)):
            ysend[r, phase + 1, n, CX - 1] = H[r, c, CX - 1, pl.ds(CY - 1, 1), :]
        send(r, phase + 1, 0)
        lax.fori_loop(0, CX - 1, body, 0)
        send(r, phase + 1, 1)

    def e_inner(r, phase):
        def body(i, carry):
            for j in range(1, TILES):
                e_tile(r, phase, i, j, False)
            return carry

        lax.fori_loop(1, CX, body, 0)

    def e_edge(r, phase):
        more = phase == 1

        def body(i, carry):
            e_tile(r, phase, i, 0, False)
            if more:
                for n, c in enumerate((0, 2)):
                    ysend[r, phase + 1, n, i] = E[r, c, i, pl.ds(0, 1), :]
            return carry

        for j in range(TILES):
            e_tile(r, phase, 0, j, True)
        if more:
            for n, c in enumerate((0, 2)):
                ysend[r, phase + 1, n, 0] = E[r, c, 0, pl.ds(0, 1), :]
            send(r, phase + 1, 0)
        lax.fori_loop(1, CX, body, 0)
        if more:
            send(r, phase + 1, 1)

    def ports(fields, t):
        plane = [fields[0, 2, 0, pl.ds(j * T, T), :] for j in range(TILES)]

        def body(n, carry):
            q = order_ref[n]
            acc = None
            for j in range(TILES):
                m = mode[q, pl.ds(j * T, T), :] * plane[j]
                acc = m if acc is None else acc + m
            total = acc[:, :ZBLK]
            for z in range(1, ZB):
                total = total + acc[:, z * ZBLK:(z + 1) * ZBLK]
            pacc[n, :, pl.ds(t * ZBLK, ZBLK)] = total
            return carry

        lax.fori_loop(0, mode.shape[0], body, 0)

    def width_copies(d):
        to = lax.rem(w + d, n_width)
        seg_c = pltpu.make_async_remote_copy(
            src_ref=seg_part.at[:, to], dst_ref=recv1.at[d - 1],
            send_sem=red_send.at[d - 1], recv_sem=red_recv.at[d - 1],
            device_id=(p, to), device_id_type=MESH)
        port_c = pltpu.make_async_remote_copy(
            src_ref=ordered.at[to], dst_ref=recvp.at[d - 1],
            send_sem=red_send.at[n_width - 1 + d - 1], recv_sem=red_recv.at[n_width - 1 + d - 1],
            device_id=(p, to), device_id_type=MESH)
        return seg_c, port_c

    pl.semaphore_wait(barrier, n_prop + n_width - 2)
    for r in range(2):
        send(r, 0, 0)
    for r in range(2):
        for c in first[r]:
            c.wait()

        def rows_out(i, carry, r=r):
            for n, c in enumerate((0, 2)):
                ysend[r, 0, n, i] = E[r, c, i, pl.ds(0, 1), :]
            return carry

        lax.fori_loop(0, CX, rows_out, 0)
        send(r, 0, 1)
    for c in rest[1] + [loads_h[1], load_mat]:
        c.start()
    for c in rest[0] + [loads_h[0]]:
        c.wait()
    h_inner(0, 0)
    load_mode.start()
    for c in rest[1] + [loads_h[1]]:
        c.wait()
    h_inner(1, 0)

    om = omega_ref[...]
    trig[0] = jnp.cos(om)
    trig[1] = jnp.cos(om * 2.0)
    trig[2] = jnp.sin(om)
    trig[3] = jnp.sin(om * 2.0)
    load_mat.wait()

    def coef_body(i, carry):
        inv = [COURANT / jnp.full((T, NZ), eps_ref[m], jnp.float32) for m in range(NMAT)]
        for j in range(TILES):
            v = mat[i, pl.ds(j * T, T), :]
            out = jnp.zeros((T, NZ), jnp.float32)
            for m in range(NMAT):
                out = jnp.where(v == m, inv[m], out)
            coef[i, pl.ds(j * T, T), :] = out
        return carry

    lax.fori_loop(0, CX, coef_body, 0)

    for phase in range(4):
        for r in range(2):
            wait_recv(r, phase, 0)
            wait_recv(r, phase, 1)
            if phase % 2 == 0:
                if phase == 2:
                    wait_send(r, 1, 0)
                h_edge(r, phase)
                e_inner(r, phase + 1)
            else:
                e_edge(r, phase)
                if phase == 1:
                    h_inner(r, phase + 1)
                elif r == 0:
                    ports(E2, 1)
                    ordered[...] = jnp.sum(pacc[...], axis=1).reshape(ordered.shape)
                    for d in range(1, n_width):
                        width_copies(d)[1].start()
        if phase == 0:
            def hot(s, carry):
                base = pl.multiple_of(s * 32, 32)
                mine = lax.broadcasted_iota(jnp.int32, (32, owner_ref.shape[1]), 0) + base
                named = owner_ref[...] * SEG_DEV + segment_ref[...]
                OH[pl.ds(base, 32), :] = jnp.where(mine == named, 1.0, 0.0).astype(jnp.bfloat16)
                return carry

            lax.fori_loop(0, OH.shape[0] // 32, hot, 0)
        if phase == 1:
            load_mode.wait()
            ports(E, 0)
    seg = None
    K = 512
    for k in range(G.shape[0] // K):
        g = G[pl.ds(k * K, K), :]
        hi = g.astype(jnp.bfloat16)
        lo = (g - hi.astype(jnp.float32)).astype(jnp.bfloat16)
        part = OH[:, pl.ds(k * K, K)]
        term = jnp.dot(part, hi, preferred_element_type=jnp.float32) + jnp.dot(part, lo, preferred_element_type=jnp.float32)
        seg = term if seg is None else seg + term
    seg_part[...] = seg.reshape(seg_part.shape)

    for d in range(1, n_width):
        width_copies(d)[0].start()

    for d in range(1, n_width):
        width_copies(d)[0].wait_recv()
    total = seg_part[:, w]
    for d in range(1, n_width):
        total = total + recv1[d - 1]
    part2[...] = total

    base = 2 * (n_width - 1)

    def prop_copy(d):
        to = lax.rem(p + d, n_prop)
        return pltpu.make_async_remote_copy(
            src_ref=part2.at[to], dst_ref=recv2.at[d - 1],
            send_sem=red_send.at[base + d - 1], recv_sem=red_recv.at[base + d - 1],
            device_id=(to, w), device_id_type=MESH)

    for d in range(1, n_prop):
        prop_copy(d).start()

    for d in range(1, n_width):
        width_copies(d)[1].wait_recv()
    mine = ordered[w]
    for d in range(1, n_width):
        mine = mine + recvp[d - 1]
    s1 = jnp.sum(mine[:, :ZBLK], axis=1, keepdims=True)
    s2 = jnp.sum(mine[:, ZBLK:], axis=1, keepdims=True)
    nf = omega_ref.shape[1]
    port_out[0, :, 0:nf] = trig[0] * s1 + trig[1] * s2
    port_out[0, :, nf:2 * nf] = -(trig[2] * s1 + trig[3] * s2)

    for d in range(1, n_prop):
        prop_copy(d).wait_recv()
    got = part2[p]
    for d in range(1, n_prop):
        got = got + recv2[d - 1]
    seg_out[...] = got

    for r in range(2):
        for phase in range(4):
            for direction in range(2):
                if (phase, direction) != (1, 0):
                    wait_send(r, phase, direction)
    for d in range(1, n_width):
        width_copies(d)[0].wait_send()
        width_copies(d)[1].wait_send()
    for d in range(1, n_prop):
        prop_copy(d).wait_send()


def write_out(E2, port, seg, ef_out, ea_out, port_out, seg_out, sem):
    pairs = ((E2.at[0], ef_out), (E2.at[1], ea_out), (port, port_out), (seg, seg_out))
    copies = [pltpu.make_async_copy(src, dst, sem.at[n]) for n, (src, dst) in enumerate(pairs)]
    for c in copies:
        c.start()
    for c in copies:
        c.wait()


def on_device(
    n_prop, n_width,
    e_forward, h_forward, e_adjoint, h_adjoint, material, eps_table, omega,
    mode_profile, port_order, owner, segment,
):
    _, CX, CY, NZ = e_forward.shape
    blocks = owner.shape[0]
    ports = mode_profile.shape[0]
    nf = omega.shape[0]
    segs = n_prop * n_width * SEG_DEV
    hbm = pl.BlockSpec(memory_space=pltpu.HBM)
    vm = pl.BlockSpec(memory_space=pltpu.VMEM)
    sm = pl.BlockSpec(memory_space=pltpu.SMEM)
    f32 = jnp.float32
    n_red = 2 * (n_width - 1) + n_prop - 1
    field = (2, 3, CX, CY, NZ)
    port_shape = (1, ports // n_width, 2 * nf)
    E2, port, seg = pl.pallas_call(
        functools.partial(kernel, n_prop, n_width),
        out_shape=(
            pltpu.VMEM(field, f32),
            pltpu.VMEM(port_shape, f32),
            pltpu.VMEM((SEG_DEV, ZBLK), f32),
        ),
        in_specs=[hbm] * 6 + [sm, vm, sm, vm, vm],
        out_specs=(vm, vm, vm),
        scratch_shapes=[
            pltpu.VMEM(field, f32),
            pltpu.VMEM(field, f32),
            pltpu.VMEM((CX, CY, NZ), jnp.int32),
            pltpu.VMEM((CX, CY, NZ), f32),
            pltpu.VMEM((ports, CY, NZ), f32),
            pltpu.VMEM((2, 4, 2, CY, NZ), f32),
            pltpu.VMEM((2, 4, 2, CX, 1, NZ), f32),
            pltpu.VMEM((2, 4, 2, CX, 1, NZ), f32),
            pltpu.VMEM((blocks, ZBLK), f32),
            pltpu.VMEM((segs, blocks), jnp.bfloat16),
            pltpu.VMEM((ports, T, 2 * ZBLK), f32),
            pltpu.VMEM((4, 1, nf), f32),
            pltpu.VMEM((n_prop, n_width, SEG_DEV, ZBLK), f32),
            pltpu.VMEM((n_width - 1, n_prop, SEG_DEV, ZBLK), f32),
            pltpu.VMEM((n_prop, SEG_DEV, ZBLK), f32),
            pltpu.VMEM((n_prop - 1, SEG_DEV, ZBLK), f32),
            pltpu.VMEM((n_width, ports // n_width, 2 * ZBLK), f32),
            pltpu.VMEM((n_width - 1, ports // n_width, 2 * ZBLK), f32),
            pltpu.SemaphoreType.DMA((14,)),
            pltpu.SemaphoreType.DMA((16,)),
            pltpu.SemaphoreType.DMA((16,)),
            pltpu.SemaphoreType.DMA((n_red,)),
            pltpu.SemaphoreType.DMA((n_red,)),
        ],
        compiler_params=pltpu.CompilerParams(
            collective_id=0, has_side_effects=True, vmem_limit_bytes=52 * 1024 * 1024
        ),
    )(
        *(pltpu.with_memory_space_constraint(x, pltpu.HBM) for x in
          (e_forward, h_forward, e_adjoint, h_adjoint, material, mode_profile)),
        eps_table, omega.reshape(1, nf), port_order, owner.reshape(1, blocks), segment.reshape(1, blocks),
    )
    return pl.pallas_call(
        write_out,
        out_shape=(
            jax.ShapeDtypeStruct(e_forward.shape, f32),
            jax.ShapeDtypeStruct(e_adjoint.shape, f32),
            jax.ShapeDtypeStruct(port_shape, f32),
            jax.ShapeDtypeStruct((SEG_DEV, ZBLK), f32),
        ),
        in_specs=[vm] * 3,
        out_specs=(hbm, hbm, hbm, hbm),
        scratch_shapes=[pltpu.SemaphoreType.DMA((4,))],
        compiler_params=pltpu.CompilerParams(vmem_limit_bytes=2 * 1024 * 1024),
    )(*(pltpu.with_memory_space_constraint(x, pltpu.VMEM) for x in (E2, port, seg)))


def solution(mesh):
    n_prop, n_width = mesh.shape["prop"], mesh.shape["width"]
    placed = (
        P(None, "prop", "width", None),
        P(None, "prop", "width", None),
        P(None, "prop", "width", None),
        P(None, "prop", "width", None),
        P("prop", "width", None),
        P(),
        P(),
        P(None, "width", None),
        P(),
        P(("prop", "width"), None),
        P(("prop", "width")),
    )
    return jax.shard_map(
        functools.partial(on_device, n_prop, n_width),
        mesh=mesh,
        in_specs=placed,
        out_specs=(
            P(None, "prop", "width", None),
            P(None, "prop", "width", None),
            P("prop", "width", None),
            P(("prop", "width"), None),
        ),
        check_vma=False,
    )
```

```python
import functools

import jax
import jax.numpy as jnp
from jax import lax
from jax.experimental import pallas as pl
from jax.experimental.pallas import tpu as pltpu
from jax.sharding import PartitionSpec as P

NMAT = 4
ZBLK = 128
SEG_DEV = 8
COURANT = 0.5
GRAD_SCALE = -0.05
MESH = pl.DeviceIdType.MESH
T = 8


def kernel(
    n_prop, n_width,
    ef_in, hf_in, ea_in, ha_in, mat_in, mode_in, eps_ref, omega_ref, order_ref, owner_ref, segment_ref,
    E2, port_out, seg_out,
    E, H, mat, coef, mode, hx_halo, hy_halo, ysend, G, OH, pacc, trig,
    seg_part, recv1, part2, recv2, ordered, recvp,
    load_sem, send_sem, recv_sem, red_send, red_recv,
):
    CX, CY, NZ = mat.shape
    TILES = CY // T
    ZB = NZ // ZBLK
    p = lax.axis_index("prop")
    w = lax.axis_index("width")
    e_in, h_in = (ef_in, ea_in), (hf_in, ha_in)

    def load(src, dst, k):
        return pltpu.make_async_copy(src, dst, load_sem.at[k])

    first = [[load(e_in[r].at[c, :, pl.ds(0, T), :], E.at[r, c, :, pl.ds(0, T), :], r * 6 + n)
              for n, c in enumerate((0, 2))] for r in range(2)]
    rest = [[load(e_in[r].at[c, :, pl.ds(T, CY - T), :], E.at[r, c, :, pl.ds(T, CY - T), :], r * 6 + 2 + n)
             for n, c in enumerate((0, 2))] + [load(e_in[r].at[1], E.at[r, 1], r * 6 + 4)] for r in range(2)]
    loads_h = [load(h_in[r], H.at[r], r * 6 + 5) for r in range(2)]
    load_mat = load(mat_in, mat, 12)
    load_mode = load(mode_in, mode, 13)
    for c in first[0] + first[1] + rest[0] + [loads_h[0]]:
        c.start()

    barrier = pltpu.get_barrier_semaphore()
    for d in range(1, n_prop):
        pl.semaphore_signal(barrier, inc=1, device_id=(lax.rem(p + d, n_prop), w), device_id_type=MESH)
    for d in range(1, n_width):
        pl.semaphore_signal(barrier, inc=1, device_id=(p, lax.rem(w + d, n_width)), device_id_type=MESH)

    def sem_of(r, phase, direction):
        return (r * 4 + phase) * 2 + direction

    def face_copy(r, phase, direction):
        ahead = phase % 2 == 0
        step = -1 if ahead else 1
        if direction == 0:
            if phase == 0:
                src = e_in[r].at[pl.ds(1, 2), 0]
            elif ahead:
                src = E.at[r, pl.ds(1, 2), 0]
            else:
                src = H.at[r, pl.ds(1, 2), CX - 1]
            dst = hx_halo.at[r, phase]
            dev = (jnp.clip(p + step, 0, n_prop - 1), w)
            may_send = p > 0 if ahead else p < n_prop - 1
            may_recv = p < n_prop - 1 if ahead else p > 0
        else:
            src = ysend.at[r, phase]
            dst = hy_halo.at[r, phase]
            dev = (p, jnp.clip(w + step, 0, n_width - 1))
            may_send = w > 0 if ahead else w < n_width - 1
            may_recv = w < n_width - 1 if ahead else w > 0
        k = sem_of(r, phase, direction)
        copy = pltpu.make_async_remote_copy(
            src_ref=src, dst_ref=dst, send_sem=send_sem.at[k], recv_sem=recv_sem.at[k],
            device_id=dev, device_id_type=MESH,
        )
        return copy, may_send, may_recv

    def send(r, phase, direction):
        copy, may_send, _ = face_copy(r, phase, direction)

        @pl.when(may_send)
        def _():
            copy.start()

    def wait_send(r, phase, direction):
        copy, may_send, _ = face_copy(r, phase, direction)

        @pl.when(may_send)
        def _():
            copy.wait_send()

    def wait_recv(r, phase, direction):
        copy, _, may_recv = face_copy(r, phase, direction)

        @pl.when(may_recv)
        def _():
            copy.wait_recv()

        @pl.when(jnp.logical_not(may_recv))
        def _():
            if direction == 0:
                hx_halo[r, phase] = jnp.zeros(hx_halo.shape[2:], jnp.float32)
            else:
                hy_halo[r, phase] = jnp.zeros(hy_halo.shape[2:], jnp.float32)

    row = lax.broadcasted_iota(jnp.int32, (T, NZ), 0)
    lane = lax.broadcasted_iota(jnp.int32, (T, NZ), 1)
    row_last, row_first = row == T - 1, row == 0
    lane_last, lane_first = lane == NZ - 1, lane == 0
    zero = jnp.float32(0.0)

    def z_next(v):
        return jnp.where(lane_last, zero, pltpu.roll(v, NZ - 1, 1))

    def z_prev(v):
        return jnp.where(lane_first, zero, pltpu.roll(v, 1, 1))

    def y_next(v, nxt):
        return jnp.where(row_last, jnp.broadcast_to(nxt, v.shape), pltpu.roll(v, T - 1, 0))

    def y_prev(v, prv):
        return jnp.where(row_first, jnp.broadcast_to(prv, v.shape), pltpu.roll(v, 1, 0))

    def h_tile(r, phase, i, j, x_edge):
        rows = pl.ds(j * T, T)
        ex, ey, ez = E[r, 0, i, rows, :], E[r, 1, i, rows, :], E[r, 2, i, rows, :]
        if x_edge:
            ey_x, ez_x = hx_halo[r, phase, 0, rows, :], hx_halo[r, phase, 1, rows, :]
        else:
            ey_x, ez_x = E[r, 1, i + 1, rows, :], E[r, 2, i + 1, rows, :]
        if j == TILES - 1:
            nx, nz = hy_halo[r, phase, 0, i], hy_halo[r, phase, 1, i]
        else:
            nx, nz = E[r, 0, i, pl.ds(j * T + T, 1), :], E[r, 2, i, pl.ds(j * T + T, 1), :]
        cx = (y_next(ez, nz) - ez) - (z_next(ey) - ey)
        cy = (z_next(ex) - ex) - (ez_x - ez)
        cz = (ey_x - ey) - (y_next(ex, nx) - ex)
        H[r, 0, i, rows, :] = H[r, 0, i, rows, :] - COURANT * cx
        H[r, 1, i, rows, :] = H[r, 1, i, rows, :] - COURANT * cy
        H[r, 2, i, rows, :] = H[r, 2, i, rows, :] - COURANT * cz

    def e_tile(r, phase, i, j, x_edge):
        rows = pl.ds(j * T, T)
        hx, hy, hz = H[r, 0, i, rows, :], H[r, 1, i, rows, :], H[r, 2, i, rows, :]
        if x_edge:
            hy_x, hz_x = hx_halo[r, phase, 0, rows, :], hx_halo[r, phase, 1, rows, :]
        else:
            hy_x, hz_x = H[r, 1, i - 1, rows, :], H[r, 2, i - 1, rows, :]
        if j == 0:
            px, pz = hy_halo[r, phase, 0, i], hy_halo[r, phase, 1, i]
        else:
            px, pz = H[r, 0, i, pl.ds(j * T - 1, 1), :], H[r, 2, i, pl.ds(j * T - 1, 1), :]
        k = coef[i, rows, :]
        old = [E[r, c, i, rows, :] for c in range(3)]
        new = [
            old[0] + k * ((hz - y_prev(hz, pz)) - (hy - z_prev(hy))),
            old[1] + k * ((hx - z_prev(hx)) - (hz - hz_x)),
            old[2] + k * ((hy - hy_x) - (hx - y_prev(hx, px))),
        ]
        out = E if phase == 1 else E2
        for c in range(3):
            out[r, c, i, rows, :] = new[c]
        if phase == 3 and r == 1:
            total = None
            for c in range(3):
                term = E[0, c, i, rows, :] * new[c] + E2[0, c, i, rows, :] * old[c]
                total = term if total is None else total + term
            g = GRAD_SCALE * total
            for z in range(ZB):
                G[pl.ds((i * CY + j * T) * ZB + z, T, stride=ZB), :] = g[:, z * ZBLK:(z + 1) * ZBLK]

    def h_inner(r, phase):
        def body(i, carry):
            for j in range(TILES - 1):
                h_tile(r, phase, i, j, False)
            return carry

        lax.fori_loop(0, CX - 1, body, 0, unroll=5)

    def h_edge(r, phase):
        def body(i, carry):
            h_tile(r, phase, i, TILES - 1, False)
            for n, c in enumerate((0, 2)):
                ysend[r, phase + 1, n, i] = H[r, c, i, pl.ds(CY - 1, 1), :]
            return carry

        for j in range(TILES):
            h_tile(r, phase, CX - 1, j, True)
        for n, c in enumerate((0, 2)):
            ysend[r, phase + 1, n, CX - 1] = H[r, c, CX - 1, pl.ds(CY - 1, 1), :]
        send(r, phase + 1, 0)
        lax.fori_loop(0, CX - 1, body, 0, unroll=5)
        send(r, phase + 1, 1)

    def e_inner(r, phase):
        def body(i, carry):
            for j in range(1, TILES):
                e_tile(r, phase, i, j, False)
            return carry

        lax.fori_loop(1, CX, body, 0, unroll=5)

    def e_edge(r, phase):
        more = phase == 1

        def body(i, carry):
            e_tile(r, phase, i, 0, False)
            if more:
                for n, c in enumerate((0, 2)):
                    ysend[r, phase + 1, n, i] = E[r, c, i, pl.ds(0, 1), :]
            return carry

        for j in range(TILES):
            e_tile(r, phase, 0, j, True)
        if more:
            for n, c in enumerate((0, 2)):
                ysend[r, phase + 1, n, 0] = E[r, c, 0, pl.ds(0, 1), :]
            send(r, phase + 1, 0)
        lax.fori_loop(1, CX, body, 0, unroll=5)
        if more:
            send(r, phase + 1, 1)

    def ports(fields, t):
        plane = [fields[0, 2, 0, pl.ds(j * T, T), :] for j in range(TILES)]

        def body(n, carry):
            q = order_ref[n]
            acc = None
            for j in range(TILES):
                m = mode[q, pl.ds(j * T, T), :] * plane[j]
                acc = m if acc is None else acc + m
            total = acc[:, :ZBLK]
            for z in range(1, ZB):
                total = total + acc[:, z * ZBLK:(z + 1) * ZBLK]
            pacc[n, :, pl.ds(t * ZBLK, ZBLK)] = total
            return carry

        lax.fori_loop(0, mode.shape[0], body, 0, unroll=4)

    def width_copies(d):
        to = lax.rem(w + d, n_width)
        seg_c = pltpu.make_async_remote_copy(
            src_ref=seg_part.at[:, to], dst_ref=recv1.at[d - 1],
            send_sem=red_send.at[d - 1], recv_sem=red_recv.at[d - 1],
            device_id=(p, to), device_id_type=MESH)
        port_c = pltpu.make_async_remote_copy(
            src_ref=ordered.at[to], dst_ref=recvp.at[d - 1],
            send_sem=red_send.at[n_width - 1 + d - 1], recv_sem=red_recv.at[n_width - 1 + d - 1],
            device_id=(p, to), device_id_type=MESH)
        return seg_c, port_c

    pl.semaphore_wait(barrier, n_prop + n_width - 2)
    for r in range(2):
        send(r, 0, 0)
    for r in range(2):
        for c in first[r]:
            c.wait()

        def rows_out(i, carry, r=r):
            for n, c in enumerate((0, 2)):
                ysend[r, 0, n, i] = E[r, c, i, pl.ds(0, 1), :]
            return carry

        lax.fori_loop(0, CX, rows_out, 0)
        send(r, 0, 1)
    for c in rest[1] + [loads_h[1], load_mat]:
        c.start()
    for c in rest[0] + [loads_h[0]]:
        c.wait()
    h_inner(0, 0)
    load_mode.start()
    for c in rest[1] + [loads_h[1]]:
        c.wait()
    h_inner(1, 0)

    om = omega_ref[...]
    trig[0] = jnp.cos(om)
    trig[1] = jnp.cos(om * 2.0)
    trig[2] = jnp.sin(om)
    trig[3] = jnp.sin(om * 2.0)
    load_mat.wait()

    def coef_body(i, carry):
        inv = [COURANT / jnp.full((T, NZ), eps_ref[m], jnp.float32) for m in range(NMAT)]
        for j in range(TILES):
            v = mat[i, pl.ds(j * T, T), :]
            out = jnp.zeros((T, NZ), jnp.float32)
            for m in range(NMAT):
                out = jnp.where(v == m, inv[m], out)
            coef[i, pl.ds(j * T, T), :] = out
        return carry

    lax.fori_loop(0, CX, coef_body, 0)

    for phase in range(4):
        for r in range(2):
            wait_recv(r, phase, 0)
            wait_recv(r, phase, 1)
            if phase % 2 == 0:
                if phase == 2:
                    wait_send(r, 1, 0)
                h_edge(r, phase)
                e_inner(r, phase + 1)
            else:
                e_edge(r, phase)
                if phase == 1:
                    h_inner(r, phase + 1)
                elif r == 0:
                    ports(E2, 1)
                    ordered[...] = jnp.sum(pacc[...], axis=1).reshape(ordered.shape)
                    for d in range(1, n_width):
                        width_copies(d)[1].start()
        if phase == 0:
            def hot(s, carry):
                base = pl.multiple_of(s * 32, 32)
                mine = lax.broadcasted_iota(jnp.int32, (32, owner_ref.shape[1]), 0) + base
                named = owner_ref[...] * SEG_DEV + segment_ref[...]
                OH[pl.ds(base, 32), :] = jnp.where(mine == named, 1.0, 0.0).astype(jnp.bfloat16)
                return carry

            lax.fori_loop(0, OH.shape[0] // 32, hot, 0)
        if phase == 1:
            load_mode.wait()
            ports(E, 0)
    seg = None
    K = 512
    for k in range(G.shape[0] // K):
        g = G[pl.ds(k * K, K), :]
        hi = g.astype(jnp.bfloat16)
        lo = (g - hi.astype(jnp.float32)).astype(jnp.bfloat16)
        part = OH[:, pl.ds(k * K, K)]
        term = jnp.dot(part, hi, preferred_element_type=jnp.float32) + jnp.dot(part, lo, preferred_element_type=jnp.float32)
        seg = term if seg is None else seg + term
    seg_part[...] = seg.reshape(seg_part.shape)

    for d in range(1, n_width):
        width_copies(d)[0].start()

    for d in range(1, n_width):
        width_copies(d)[0].wait_recv()
    total = seg_part[:, w]
    for d in range(1, n_width):
        total = total + recv1[d - 1]
    part2[...] = total

    base = 2 * (n_width - 1)

    def prop_copy(d):
        to = lax.rem(p + d, n_prop)
        return pltpu.make_async_remote_copy(
            src_ref=part2.at[to], dst_ref=recv2.at[d - 1],
            send_sem=red_send.at[base + d - 1], recv_sem=red_recv.at[base + d - 1],
            device_id=(to, w), device_id_type=MESH)

    for d in range(1, n_prop):
        prop_copy(d).start()

    for d in range(1, n_width):
        width_copies(d)[1].wait_recv()
    mine = ordered[w]
    for d in range(1, n_width):
        mine = mine + recvp[d - 1]
    s1 = jnp.sum(mine[:, :ZBLK], axis=1, keepdims=True)
    s2 = jnp.sum(mine[:, ZBLK:], axis=1, keepdims=True)
    nf = omega_ref.shape[1]
    port_out[0, :, 0:nf] = trig[0] * s1 + trig[1] * s2
    port_out[0, :, nf:2 * nf] = -(trig[2] * s1 + trig[3] * s2)

    for d in range(1, n_prop):
        prop_copy(d).wait_recv()
    got = part2[p]
    for d in range(1, n_prop):
        got = got + recv2[d - 1]
    seg_out[...] = got

    for r in range(2):
        for phase in range(4):
            for direction in range(2):
                if (phase, direction) != (1, 0):
                    wait_send(r, phase, direction)
    for d in range(1, n_width):
        width_copies(d)[0].wait_send()
        width_copies(d)[1].wait_send()
    for d in range(1, n_prop):
        prop_copy(d).wait_send()


def write_out(E2, port, seg, ef_out, ea_out, port_out, seg_out, sem):
    pairs = ((E2.at[0], ef_out), (E2.at[1], ea_out), (port, port_out), (seg, seg_out))
    copies = [pltpu.make_async_copy(src, dst, sem.at[n]) for n, (src, dst) in enumerate(pairs)]
    for c in copies:
        c.start()
    for c in copies:
        c.wait()


def on_device(
    n_prop, n_width,
    e_forward, h_forward, e_adjoint, h_adjoint, material, eps_table, omega,
    mode_profile, port_order, owner, segment,
):
    _, CX, CY, NZ = e_forward.shape
    blocks = owner.shape[0]
    ports = mode_profile.shape[0]
    nf = omega.shape[0]
    segs = n_prop * n_width * SEG_DEV
    hbm = pl.BlockSpec(memory_space=pltpu.HBM)
    vm = pl.BlockSpec(memory_space=pltpu.VMEM)
    sm = pl.BlockSpec(memory_space=pltpu.SMEM)
    f32 = jnp.float32
    n_red = 2 * (n_width - 1) + n_prop - 1
    field = (2, 3, CX, CY, NZ)
    port_shape = (1, ports // n_width, 2 * nf)
    E2, port, seg = pl.pallas_call(
        functools.partial(kernel, n_prop, n_width),
        out_shape=(
            pltpu.VMEM(field, f32),
            pltpu.VMEM(port_shape, f32),
            pltpu.VMEM((SEG_DEV, ZBLK), f32),
        ),
        in_specs=[hbm] * 6 + [sm, vm, sm, vm, vm],
        out_specs=(vm, vm, vm),
        scratch_shapes=[
            pltpu.VMEM(field, f32),
            pltpu.VMEM(field, f32),
            pltpu.VMEM((CX, CY, NZ), jnp.int32),
            pltpu.VMEM((CX, CY, NZ), f32),
            pltpu.VMEM((ports, CY, NZ), f32),
            pltpu.VMEM((2, 4, 2, CY, NZ), f32),
            pltpu.VMEM((2, 4, 2, CX, 1, NZ), f32),
            pltpu.VMEM((2, 4, 2, CX, 1, NZ), f32),
            pltpu.VMEM((blocks, ZBLK), f32),
            pltpu.VMEM((segs, blocks), jnp.bfloat16),
            pltpu.VMEM((ports, T, 2 * ZBLK), f32),
            pltpu.VMEM((4, 1, nf), f32),
            pltpu.VMEM((n_prop, n_width, SEG_DEV, ZBLK), f32),
            pltpu.VMEM((n_width - 1, n_prop, SEG_DEV, ZBLK), f32),
            pltpu.VMEM((n_prop, SEG_DEV, ZBLK), f32),
            pltpu.VMEM((n_prop - 1, SEG_DEV, ZBLK), f32),
            pltpu.VMEM((n_width, ports // n_width, 2 * ZBLK), f32),
            pltpu.VMEM((n_width - 1, ports // n_width, 2 * ZBLK), f32),
            pltpu.SemaphoreType.DMA((14,)),
            pltpu.SemaphoreType.DMA((16,)),
            pltpu.SemaphoreType.DMA((16,)),
            pltpu.SemaphoreType.DMA((n_red,)),
            pltpu.SemaphoreType.DMA((n_red,)),
        ],
        compiler_params=pltpu.CompilerParams(
            collective_id=0, has_side_effects=True, vmem_limit_bytes=52 * 1024 * 1024
        ),
    )(
        *(pltpu.with_memory_space_constraint(x, pltpu.HBM) for x in
          (e_forward, h_forward, e_adjoint, h_adjoint, material, mode_profile)),
        eps_table, omega.reshape(1, nf), port_order, owner.reshape(1, blocks), segment.reshape(1, blocks),
    )
    return pl.pallas_call(
        write_out,
        out_shape=(
            jax.ShapeDtypeStruct(e_forward.shape, f32),
            jax.ShapeDtypeStruct(e_adjoint.shape, f32),
            jax.ShapeDtypeStruct(port_shape, f32),
            jax.ShapeDtypeStruct((SEG_DEV, ZBLK), f32),
        ),
        in_specs=[vm] * 3,
        out_specs=(hbm, hbm, hbm, hbm),
        scratch_shapes=[pltpu.SemaphoreType.DMA((4,))],
        compiler_params=pltpu.CompilerParams(vmem_limit_bytes=2 * 1024 * 1024),
    )(*(pltpu.with_memory_space_constraint(x, pltpu.VMEM) for x in (E2, port, seg)))


def solution(mesh):
    n_prop, n_width = mesh.shape["prop"], mesh.shape["width"]
    placed = (
        P(None, "prop", "width", None),
        P(None, "prop", "width", None),
        P(None, "prop", "width", None),
        P(None, "prop", "width", None),
        P("prop", "width", None),
        P(),
        P(),
        P(None, "width", None),
        P(),
        P(("prop", "width"), None),
        P(("prop", "width")),
    )
    return jax.shard_map(
        functools.partial(on_device, n_prop, n_width),
        mesh=mesh,
        in_specs=placed,
        out_specs=(
            P(None, "prop", "width", None),
            P(None, "prop", "width", None),
            P("prop", "width", None),
            P(("prop", "width"), None),
        ),
        check_vma=False,
    )
```
